256 devices in a mesh: comp: 4 (over y), gx: 16 (over z_hi, x), gy: 4 (over z_lo, core).
Axes of the slice: x: 4, y: 4, z: 8 (z_hi: 4, z_lo: 2; z = z_hi * 2 + z_lo), core: 2. Of those that a mesh axis runs over, the one named last changes fastest.
Arguments:
- state: float32 [32, 256, 128, 128], P('comp', 'gx', 'gy'), may hold values from -4 to 4
- levels: int32 [256, 128], P('gx', 'gy'), may hold values from 0 to 128
- reaction: float32 [3, 8, 8], replicated, may hold values from -2 to 2
Outputs:
- new_state: float32 [32, 256, 128, 128], P('comp', 'gx', 'gy')
The draws below stay inside these ranges and needn't reach their ends.
Inputs may be any that keep to these rules, and one draw needn't show every extreme that they name: `levels`: 0 marks a land column, 128 a column of full depth.
All inputs are finite; a program needn't handle non-finite values.
Results may differ from the reference program's by a relative error of at most 0.00018.
Values sent between devices are 32-bit elements; how exact they have to be, the bound alone decides.
A program may use at most 64 MiB of HBM per device.

```python
import jax
import jax.numpy as jnp
from jax import lax

NF = 8
NZ = 128
ITERS = 3
NFIELDS = 32
NX = 256
NY = 128
N_COMP = 4


def plant(entries, stream_key, low, largest):
    index_at = [jax.random.randint(jax.random.fold_in(stream_key, axis), (), 0, length) for axis, length in enumerate(entries.shape)]
    main_axis = entries.shape.index(max(entries.shape))
    next_to = index_at[:main_axis] + [(index_at[main_axis] + 1) % entries.shape[main_axis]] + index_at[main_axis + 1:]
    return entries.at[tuple(index_at)].set(low).at[tuple(next_to)].set(largest)


def block_levels(stream_key, extent, cuts, least, high):
    loudness, own = 1.0, jax.random.fold_in(stream_key, 6)
    for position, shards_of in cuts:
        steps = jnp.exp(jax.random.uniform(jax.random.fold_in(own, position), (shards_of,), jnp.float32, least / len(cuts), high / len(cuts)))
        loudness = loudness * jnp.repeat(steps, extent[position] // shards_of).reshape([-1 if axis == position else 1 for axis in range(len(extent))])
    return loudness


def noise(key, shape, spread, most, cuts=(), held_as=jnp.bfloat16):
    drawn = jax.random.normal(key, shape, jnp.float32) * spread
    if len(cuts) > 0:
        drawn = block_levels(key, shape, cuts, -0.22, 0.18) * drawn
    return jnp.clip(drawn, min=-most, max=most).astype(held_as)


def setup_inputs(seed: int = 0) -> dict:
    seeds = jax.random.split(jax.random.key(seed), 4)
    state = noise(seeds[0], (NFIELDS, NX, NY, NZ), 0.7, 4.0, ((0, 4), (1, 16), (2, 4)), jnp.float32)
    levels = plant(jax.random.randint(seeds[1], (NX, NY), 0, NZ + 1), jax.random.fold_in(seeds[1], 1), 0, NZ).astype(jnp.int32)
    reaction = noise(seeds[2], (N_COMP - 1, NF, NF), NF ** -0.5, 2.0, (), jnp.float32)
    return dict(state=state, levels=levels, reaction=reaction)


time_step = 0.25
lateral_mix = 0.05
vertical_mix = 0.1
pressure_scale = 0.05
thermal_coef = 1.0
haline_coef = 0.8
coriolis_mean = 0.5
coriolis_slope = 0.5


def along(padded, axis, shift):
    count_x = padded.shape[1] - 4
    count_y = padded.shape[2] - 4
    if axis == 1:
        return padded[:, 2 + shift:2 + shift + count_x, 2:2 + count_y]
    return padded[:, 2:2 + count_x, 2 + shift:2 + shift + count_y]


def centered(padded, axis):
    return (8.0 * (along(padded, axis, 1) - along(padded, axis, -1)) - (along(padded, axis, 2) - along(padded, axis, -2))) / 12.0


def smoothing(padded, axis):
    return (along(padded, axis, 2) + along(padded, axis, -2) - 4.0 * (along(padded, axis, 1) + along(padded, axis, -1)) + 6.0 * along(padded, axis, 0)) / 12.0


def transport(padded, east, north):
    return east * centered(padded, 1) + jnp.abs(east) * smoothing(padded, 1) + north * centered(padded, 2) + jnp.abs(north) * smoothing(padded, 2)


def lateral(padded):
    return along(padded, 1, 1) + along(padded, 1, -1) + along(padded, 2, 1) + along(padded, 2, -1) - 4.0 * along(padded, 1, 0)


def vertical(center):
    column = jnp.pad(center, ((0, 0), (0, 0), (0, 0), (1, 1)))
    return column[..., 2:] + column[..., :-2] - 2.0 * center


def dynamics_step(padded, mask, latitude, accumulate):
    center = padded[:, 2:-2, 2:-2]
    east = center[0]
    north = center[1]
    moving = padded[0:4]
    density = haline_coef * padded[3] - thermal_coef * padded[2]
    pressure = (pressure_scale * accumulate(density))[None]
    tendency = lateral_mix * lateral(moving) + vertical_mix * vertical(center[0:4]) - transport(moving, east, north)
    rotation = (coriolis_mean + coriolis_slope * latitude)[None, :, None]
    push_east = tendency[0] + rotation * north - centered(pressure, 1)[0]
    push_north = tendency[1] - rotation * east - centered(pressure, 2)[0]
    tendency = jnp.stack([push_east, push_north, tendency[2], tendency[3]])
    advanced = center[0:4] + time_step * (1.5 * tendency - 0.5 * center[4:8])
    return jnp.concatenate([advanced * mask, tendency * mask])


def tracer_step(padded, velocity, mask, coupling):
    center = padded[:, 2:-2, 2:-2]
    growth = 2.0 * jax.nn.sigmoid(velocity[2])
    reacting = growth * jnp.einsum("ij,jxyz->ixyz", coupling, center, precision=lax.Precision.HIGHEST)
    tendency = lateral_mix * lateral(padded) + vertical_mix * vertical(center) + reacting - transport(padded, velocity[0], velocity[1])
    return (center + time_step * tendency) * mask


def running_sum(density):
    return jnp.cumsum(density, axis=-1)


def pad_group(group):
    wrapped = jnp.pad(group, ((0, 0), (2, 2), (0, 0), (0, 0)), mode="wrap")
    return jnp.pad(wrapped, ((0, 0), (0, 0), (2, 2), (0, 0)))


def reference(state, levels, reaction):
    depth = jnp.arange(NZ).astype(jnp.int32)
    mask = (depth[None, None, :] < levels[:, :, None]).astype(jnp.float32)
    latitude = 2.0 * jnp.arange(NY).astype(jnp.float32) / (NY - 1) - 1.0
    for step in range(ITERS):
        state = state * mask[None]
        velocity = state[0:3]
        pieces = [dynamics_step(pad_group(state[0:NF]), mask, latitude, running_sum)]
        for group in range(N_COMP - 1):
            block = state[NF * (group + 1):NF * (group + 2)]
            pieces.append(tracer_step(pad_group(block), velocity, mask, reaction[group]))
        state = jnp.concatenate(pieces)
    return state
```

```python
import functools

import jax
import jax.numpy as jnp
from jax import lax
from jax.experimental import pallas as pl
from jax.experimental.pallas import tpu as pltpu
from jax.sharding import PartitionSpec as P

MESH = pl.DeviceIdType.MESH
ITERS = 3
EDGE = 8
X_CHIPS = 4
LAG = 4

time_step = 0.25
lateral_mix = 0.05
vertical_mix = 0.1
pressure_scale = 0.05
thermal_coef = 1.0
haline_coef = 0.8
coriolis_mean = 0.5
coriolis_slope = 0.5


def weights(speed, scale):
    size = jnp.abs(speed)
    mix = scale * lateral_mix
    eight = speed * (scale * 8.0 / 12.0)
    four = size * (scale * 4.0 / 12.0) + mix
    return four - eight, four + eight, (speed - size) * (scale / 12.0), (speed + size) * (-scale / 12.0)


def kernel(
    mesh_size, state_ref, levels_ref, reaction_ref, out_ref, pad, vel, mask, mixing, summing, slope, push,
    load_sem, out_sem, vel_send, vel_recv, x_send, x_recv, y_send, y_recv,
):
    count_gx, count_gy = mesh_size
    fields, rows, cells_y, depth = state_ref.shape
    pairs = rows // 2
    tiles = cells_y // 8
    slot = lax.axis_index("comp")
    gx = lax.axis_index("gx")
    gy = lax.axis_index("gy")
    east = lax.rem(gx + 1, count_gx)
    west = lax.rem(gx + count_gx - 1, count_gx)
    south = lax.rem(gy + 1, count_gy)
    north = lax.rem(gy + count_gy - 1, count_gy)
    inside = pl.ds(EDGE, cells_y)

    def load(j, first, size):
        return pltpu.make_async_copy(
            state_ref.at[:, pl.ds(first, size)], pad.at[0, :, pl.ds(2 + first, size), inside], load_sem.at[j]
        )

    loads = [load(0, 0, 2), load(1, rows - 2, 2), load(2, 2, rows - 4)]
    for copy in loads:
        copy.start()

    barrier = pltpu.get_barrier_semaphore()
    for near in (
        {"gx": east}, {"gx": west}, {"gy": south}, {"gy": north},
        {"comp": lax.rem(slot + 1, 4)}, {"comp": lax.rem(slot + 3, 4)},
    ):
        pl.semaphore_signal(barrier, inc=1, device_id=near, device_id_type=MESH)

    lane = lax.broadcasted_iota(jnp.int32, (8, depth), 1)
    own_y = lax.broadcasted_iota(jnp.int32, (8, cells_y), 0)
    at_y = lax.broadcasted_iota(jnp.int32, (8, cells_y), 1)
    lanes = lane.astype(jnp.float32)
    for row in range(rows):
        level = jnp.broadcast_to(levels_ref[pl.ds(row, 1), :], (8, cells_y)).astype(jnp.float32)
        for t in range(tiles):
            column = jnp.sum(jnp.where(at_y == own_y + 8 * t, level, 0.0), axis=1, keepdims=True)
            mask[row, pl.ds(8 * t, 8)] = jnp.where(lanes < column, 1.0, 0.0)

    def wall(first):
        zeros = jnp.zeros((8, depth), jnp.float32)

        @pl.loop(0, rows)
        def _(row):
            for step in range(ITERS):
                for f in range(fields):
                    pad[step, f, 2 + row, pl.ds(first, 8)] = zeros

    pl.when(gy == 0)(lambda: wall(0))
    pl.when(gy == count_gy - 1)(lambda: wall(EDGE + cells_y))

    up = jnp.where(lane > 0, 1.0, 0.0)
    down = jnp.where(lane < depth - 1, 1.0, 0.0)

    def cover(row):
        for f in range(fields):
            pad[0, f, 2 + row, inside] = pad[0, f, 2 + row, inside] * mask[row]

    def send_x(step, j, kinds):
        for side, row, to_row, to in ((0, j, rows + j, west), (1, rows - 1 - j, -1 - j, east)):
            pltpu.make_async_remote_copy(
                src_ref=pad.at[step, pl.ds(0, kinds), 2 + row, inside],
                dst_ref=pad.at[step, pl.ds(0, kinds), 2 + to_row, inside],
                send_sem=x_send.at[step, side, j],
                recv_sem=x_recv.at[step, side, j],
                device_id={"gx": to},
                device_id_type=MESH,
            ).start()

    def end_x(step, j, kinds, sent):
        for side in range(2):
            block = pad.at[step, pl.ds(0, kinds), 2, inside]
            copy = pltpu.make_async_remote_copy(
                src_ref=block, dst_ref=block, send_sem=x_send.at[step, side, j], recv_sem=x_recv.at[step, side, j],
                device_id={"gx": east}, device_id_type=MESH,
            )
            copy.wait_send() if sent else copy.wait_recv()

    def y_copies(step, j, kinds):
        for group in (j, pairs - 1 - j):
            for side, first, to_first, to in ((0, EDGE, EDGE + cells_y, north), (1, EDGE + cells_y - 2, EDGE - 2, south)):
                yield side, pltpu.make_async_remote_copy(
                    src_ref=pad.at[step, pl.ds(0, kinds), pl.ds(2 + 2 * group, 2), pl.ds(first, 2)],
                    dst_ref=pad.at[step, pl.ds(0, kinds), pl.ds(2 + 2 * group, 2), pl.ds(to_first, 2)],
                    send_sem=y_send.at[step, side, group],
                    recv_sem=y_recv.at[step, side, group],
                    device_id={"gy": to},
                    device_id_type=MESH,
                )

    def send_y(step, j, kinds):
        for side, copy in y_copies(step, j, kinds):
            pl.when(gy > 0 if side == 0 else gy < count_gy - 1)(copy.start)

    def end_y(step, j, kinds, sent):
        for side, copy in y_copies(step, j, kinds):
            if sent:
                pl.when(gy > 0 if side == 0 else gy < count_gy - 1)(copy.wait_send)
            else:
                pl.when(gy < count_gy - 1 if side == 0 else gy > 0)(copy.wait_recv)

    def write(j):
        for group in (j, pairs - 1 - j):
            yield pltpu.make_async_copy(
                pad.at[ITERS, :, pl.ds(2 + 2 * group, 2), inside], out_ref.at[:, pl.ds(2 * group, 2)], out_sem.at[group]
            )

    def vel_copy(step, row, source, to):
        return pltpu.make_async_remote_copy(
            src_ref=source,
            dst_ref=vel.at[step, :, row],
            send_sem=vel_send.at[step, row],
            recv_sem=vel_recv.at[step, row],
            device_id={"comp": to},
            device_id_type=MESH,
        )

    def send_vel(step, k):
        for row, to in ((k, 1), (rows - 1 - k, 3)):
            vel_copy(step, row, pad.at[step, pl.ds(0, 3), 2 + row, inside], to).start()

    def start(kinds, feeds):
        for j in range(2):
            loads[j].wait()
        for row in (0, rows - 1, 1, rows - 2):
            cover(row)
        pl.semaphore_wait(barrier, 6)
        for j in range(2):
            if feeds:
                send_vel(0, j)
            send_x(0, j, kinds)
        send_y(0, 0, kinds)
        loads[2].wait()

        @pl.loop(1, pairs // 2)
        def _(j):
            for k in (2 * j, 2 * j + 1):
                cover(k)
                cover(rows - 1 - k)
            if feeds:
                send_vel(0, 2 * j)
                send_vel(0, 2 * j + 1)
            send_y(0, j, kinds)

    def each_pair(kinds, compute, after):
        @pl.loop(0, ITERS * pairs)
        def _(n):
            step = n // pairs
            k = n % pairs
            odd = k % 2

            @pl.when(k == 0)
            def _():
                for j in range(2):
                    end_x(step, j, kinds, False)

            @pl.when(odd == 0)
            def _():
                end_y(step, k // 2, kinds, False)

            compute(n, step, k)

            @pl.when(step < ITERS - 1)
            def _():
                after(step + 1, k)

                @pl.when(k < 2)
                def _():
                    send_x(step + 1, k, kinds)

                @pl.when(odd == 1)
                def _():
                    send_y(step + 1, k // 2, kinds)

            @pl.when((step == ITERS - 1) & (odd == 1))
            def _():
                for copy in write(k // 2):
                    copy.start()

        @pl.loop(0, ITERS)
        def _(step):
            for j in range(2):
                end_x(step, j, kinds, True)

            @pl.loop(0, pairs // 2)
            def _(j):
                end_y(step, j, kinds, True)

        for j in range(pairs // 2):
            for copy in write(j):
                copy.wait()

    def turn(q, by):
        return pltpu.roll(q, by % depth, 1)

    def cell(step, f, x, t, shift=0):
        return pad[step, f, x, pl.ds(EDGE + 8 * t + shift, 8)]

    def density_slopes(step, row, at):
        x = row + 2
        scale = pressure_scale / 12.0

        def difference(f, t, along_x):
            if along_x:
                one, two = cell(step, f, x + 1, t) - cell(step, f, x - 1, t), cell(step, f, x + 2, t) - cell(step, f, x - 2, t)
            else:
                one, two = cell(step, f, x, t, 1) - cell(step, f, x, t, -1), cell(step, f, x, t, 2) - cell(step, f, x, t, -2)
            return 8.0 * one - two

        for t in range(tiles):
            for way, along_x in enumerate((True, False)):
                salt, heat = difference(3, t, along_x), difference(2, t, along_x)
                slope[pl.ds(at + (way * tiles + t) * 8, 8)] = (scale * haline_coef) * salt - (scale * thermal_coef) * heat

    def dynamics_row(step, row, at):
        x = row + 2
        for t in range(tiles):
            u, v = cell(step, 0, x, t), cell(step, 1, x, t)
            m = mask[row, pl.ds(8 * t, 8)]
            along_x, along_y = weights(u, 1.0), weights(v, 1.0)
            middle = -0.5 * (jnp.abs(u) + jnp.abs(v)) - (4.0 * lateral_mix + 2.0 * vertical_mix)
            y = gy * cells_y + 8 * t + lax.broadcasted_iota(jnp.int32, (8, depth), 0)
            latitude = 2.0 * y.astype(jnp.float32) / float(cells_y * count_gy - 1) - 1.0
            spin = coriolis_mean + coriolis_slope * latitude
            for f in range(4):
                q = cell(step, f, x, t)
                total = middle * q
                for w, shift in zip(along_x, (1, -1, 2, -2)):
                    total += w * cell(step, f, x + shift, t)
                for w, shift in zip(along_y, (1, -1, 2, -2)):
                    total += w * cell(step, f, x, t, shift)
                total += (vertical_mix * up) * turn(q, 1) + (vertical_mix * down) * turn(q, -1)
                if f == 0:
                    total += spin * v - push[pl.ds(at + t * 8, 8)]
                if f == 1:
                    total -= spin * u + push[pl.ds(at + (tiles + t) * 8, 8)]
                before = cell(step, 4 + f, x, t)
                pad[step + 1, f, x, pl.ds(EDGE + 8 * t, 8)] = m * (
                    q + ((1.5 * time_step) * total - (0.5 * time_step) * before)
                )
                pad[step + 1, 4 + f, x, pl.ds(EDGE + 8 * t, 8)] = m * total

    def run_dynamics():
        above = lax.broadcasted_iota(jnp.int32, (depth, depth), 0)
        below = lax.broadcasted_iota(jnp.int32, (depth, depth), 1)
        summing[...] = jnp.where(above <= below, 1.0, 0.0)
        start(4, True)

        def compute(n, step, k):
            density_slopes(step, k, 0)
            density_slopes(step, rows - 1 - k, 2 * cells_y)
            push[...] = jnp.dot(
                slope[...], summing[...], precision=lax.Precision.HIGHEST, preferred_element_type=jnp.float32
            )
            dynamics_row(step, k, 0)
            dynamics_row(step, rows - 1 - k, 2 * cells_y)

        each_pair(4, compute, send_vel)

        @pl.loop(0, ITERS)
        def _(step):
            @pl.loop(0, rows)
            def _(row):
                vel_copy(step, row, vel.at[step, :, row], 1).wait_send()

    def tracer_row(step, row):
        x = row + 2
        for t0 in range(0, tiles, 2):
            here = []
            for t in (t0, t0 + 1):
                at = pl.ds(8 * t, 8)
                u, v, heat = vel[step, 0, row, at], vel[step, 1, row, at], vel[step, 2, row, at]
                along_x, along_y = weights(u, time_step), weights(v, time_step)
                middle = (-0.5 * time_step) * (jnp.abs(u) + jnp.abs(v)) + (
                    1.0 - time_step * (4.0 * lateral_mix + 2.0 * vertical_mix)
                )
                growth = (2.0 * time_step) * jax.nn.sigmoid(heat)
                q = [cell(step, f, x, t) for f in range(fields)]
                here.append((t, mask[row, at], along_x, along_y, middle, growth, q))
            for f in range(fields):
                rates = [mixing[f, j] for j in range(fields)]
                for t, m, along_x, along_y, middle, growth, q in here:
                    reacting = rates[0] * q[0]
                    for j in range(1, fields):
                        reacting += rates[j] * q[j]
                    total = middle * q[f] + growth * reacting
                    for w, shift in zip(along_x, (1, -1, 2, -2)):
                        total += w * cell(step, f, x + shift, t)
                    for w, shift in zip(along_y, (1, -1, 2, -2)):
                        total += w * cell(step, f, x, t, shift)
                    total += (time_step * vertical_mix * up) * turn(q[f], 1) + (time_step * vertical_mix * down) * turn(q[f], -1)
                    pad[step + 1, f, x, pl.ds(EDGE + 8 * t, 8)] = m * total

    def run_tracers():
        for i in range(fields):
            for j in range(fields):
                mixing[i, j] = jnp.full((8, depth), reaction_ref[slot - 1, i, j], jnp.float32)
        start(fields, False)
        total = ITERS * pairs
        ahead = LAG * (3 - slot) // 2
        behind = LAG * (slot - 1) // 2

        def relay(c, row, last, to):
            copy = vel_copy(c // pairs, row, vel.at[c // pairs, :, row], to)
            copy.wait_recv()
            pl.when(last)(copy.start)

        def going_up(c):
            relay(c, c % pairs, slot < 3, lax.rem(slot + 1, 4))

        def going_down(c):
            relay(c, rows - 1 - c % pairs, slot > 1, slot - 1)

        @pl.loop(0, ahead)
        def _(c):
            going_up(c)

        @pl.loop(0, behind)
        def _(c):
            going_down(c)

        def compute(n, step, k):
            pl.when(n + ahead < total)(lambda: going_up(n + ahead))
            pl.when(n + behind < total)(lambda: going_down(n + behind))
            tracer_row(step, k)
            tracer_row(step, rows - 1 - k)

        each_pair(fields, compute, lambda step, k: None)

        @pl.loop(0, total)
        def _(c):
            step = c // pairs
            k = c % pairs
            pl.when(slot < 3)(lambda: vel_copy(step, k, vel.at[step, :, k], 1).wait_send())
            pl.when(slot > 1)(lambda: vel_copy(step, rows - 1 - k, vel.at[step, :, k], 1).wait_send())

    pl.when(slot == 0)(run_dynamics)
    pl.when(slot != 0)(run_tracers)


def solution(mesh):
    mesh_size = (mesh.shape["gx"], mesh.shape["gy"])

    def per_device(state, levels, reaction):
        fields, rows, cells_y, depth = state.shape
        dma = pltpu.SemaphoreType.DMA
        padded = (fields, rows + 4, cells_y + 2 * EDGE, depth)
        return pl.pallas_call(
            functools.partial(kernel, mesh_size),
            out_shape=jax.ShapeDtypeStruct(state.shape, state.dtype),
            in_specs=[
                pl.BlockSpec(memory_space=pl.ANY),
                pl.BlockSpec(memory_space=pltpu.VMEM),
                pl.BlockSpec(memory_space=pltpu.SMEM),
            ],
            out_specs=pl.BlockSpec(memory_space=pl.ANY),
            scratch_shapes=[
                pltpu.VMEM((ITERS + 1, *padded), jnp.float32),
                pltpu.VMEM((ITERS, 3, rows, cells_y, depth), jnp.float32),
                pltpu.VMEM((rows, cells_y, depth), jnp.float32),
                pltpu.VMEM((fields, fields, 8, depth), jnp.float32),
                pltpu.VMEM((depth, depth), jnp.float32),
                pltpu.VMEM((4 * cells_y, depth), jnp.float32),
                pltpu.VMEM((4 * cells_y, depth), jnp.float32),
                dma((3,)),
                dma((rows // 2,)),
                dma((ITERS, rows)),
                dma((ITERS, rows)),
                dma((ITERS, 2, 2)),
                dma((ITERS, 2, 2)),
                dma((ITERS, 2, rows // 2)),
                dma((ITERS, 2, rows // 2)),
            ],
            compiler_params=pltpu.CompilerParams(
                collective_id=0, has_side_effects=True, vmem_limit_bytes=32 * 1024 * 1024
            ),
        )(state, levels, reaction)

    in_specs = (P("comp", "gx", "gy", None), P("gx", "gy"), P())
    out_specs = P("comp", "gx", "gy", None)
    return jax.shard_map(per_device, mesh=mesh, in_specs=in_specs, out_specs=out_specs, check_vma=False)
```

```python
import functools

import jax
import jax.numpy as jnp
from jax import lax
from jax.experimental import pallas as pl
from jax.experimental.pallas import tpu as pltpu
from jax.sharding import PartitionSpec as P

MESH = pl.DeviceIdType.MESH
ITERS = 3
EDGE = 8
X_CHIPS = 4
LAG = 8
QUARTERS = 3
HAND_ON = tuple((0, p, 0, 0) for p in range(QUARTERS)) + ((1, 0, 0, 3), (1, 1, 0, 4), (1, 2, 0, 5), (2, 0, 1, 7), (2, 1, 2, 0), (2, 2, 2, 1))

time_step = 0.25
lateral_mix = 0.05
vertical_mix = 0.1
pressure_scale = 0.05
thermal_coef = 1.0
haline_coef = 0.8
coriolis_mean = 0.5
coriolis_slope = 0.5


def weights(speed, scale):
    size = jnp.abs(speed)
    mix = scale * lateral_mix
    eight = speed * (scale * 8.0 / 12.0)
    four = size * (scale * 4.0 / 12.0) + mix
    return four - eight, four + eight, (speed - size) * (scale / 12.0), (speed + size) * (-scale / 12.0)


def halves(value):
    high = value.astype(jnp.bfloat16)
    return high, (value - high.astype(jnp.float32)).astype(jnp.bfloat16)


def kernel(
    mesh_size, state_ref, levels_ref, reaction_ref, out_ref, pad0, pad1, pad2, vel, mask, level, mixing, rates, summing, slope,
    push, detour, coupling, load_sem, vel_send, vel_recv, x_send, x_recv, y_send, y_recv, detour_recv, detour_send,
):
    count_gx, count_gy = mesh_size
    pads = (pad0, pad1, pad2)
    fields, rows, cells_y, depth = state_ref.shape
    pairs = rows // 2
    tiles = cells_y // 8
    slot = lax.axis_index("comp")
    gx = lax.axis_index("gx")
    gy = lax.axis_index("gy")

    def along(by):
        return {"gx": lax.rem(gx + (count_gx + by), count_gx)}

    east, west = along(1), along(-1)
    south = {"gy": lax.rem(gy + 1, count_gy)}
    north = {"gy": lax.rem(gy + count_gy - 1, count_gy)}
    chip = lax.rem(gx, X_CHIPS)
    first_chip, last_chip = chip == 0, chip == X_CHIPS - 1
    inside = pl.ds(EDGE, cells_y)

    def load(j, first, size):
        return pltpu.make_async_copy(
            state_ref.at[:, pl.ds(first, size)], pad0.at[:, pl.ds(2 + first, size), inside], load_sem.at[j]
        )

    loads = [load(0, 0, 2), load(1, rows - 2, 2), load(2, 2, rows - 4)]
    small = [
        pltpu.make_async_copy(levels_ref, level, load_sem.at[3]),
        pltpu.make_async_copy(reaction_ref, coupling, load_sem.at[4]),
    ]
    for copy in small + loads:
        copy.start()

    barrier = pltpu.get_barrier_semaphore()
    nearby = [along(by) for by in (1, -1, X_CHIPS, -X_CHIPS, X_CHIPS - 1, 1 - X_CHIPS)]
    nearby += [south, north, {"comp": lax.rem(slot + 1, 4)}, {"comp": lax.rem(slot + 3, 4)}]
    for near in nearby:
        pl.semaphore_signal(barrier, inc=1, device_id=near, device_id_type=MESH)

    lane = lax.broadcasted_iota(jnp.int32, (8, depth), 1)
    own_y = lax.broadcasted_iota(jnp.int32, (8, cells_y), 0)
    at_y = lax.broadcasted_iota(jnp.int32, (8, cells_y), 1)
    lanes = lane.astype(jnp.float32)
    def set_mask(row):
        here = jnp.broadcast_to(level[pl.ds(row, 1), :], (8, cells_y)).astype(jnp.float32)
        for t in range(tiles):
            column = jnp.sum(jnp.where(at_y == own_y + 8 * t, here, 0.0), axis=1, keepdims=True)
            mask[row, pl.ds(8 * t, 8)] = jnp.where(lanes < column, 1.0, 0.0)

    for copy in small:
        copy.wait()
    for row in (0, rows - 1, 1, rows - 2):
        set_mask(row)

    def wall(first):
        zeros = jnp.zeros((8, depth), jnp.float32)

        @pl.loop(0, rows)
        def _(row):
            for pad in pads:
                for f in range(fields):
                    pad[f, 2 + row, pl.ds(first, 8)] = zeros

    def neighbours_above_below(scale):
        up = jnp.where(lane > 0, scale, 0.0)
        down = jnp.where(lane < depth - 1, scale, 0.0)
        return lambda q: up * pltpu.roll(q, 1, 1) + down * pltpu.roll(q, depth - 1, 1)

    def cover(row):
        for f in range(fields):
            pad0[f, 2 + row, inside] = pad0[f, 2 + row, inside] * mask[row]

    def remote(source, target, send, recv, to):
        return pltpu.make_async_remote_copy(
            src_ref=source, dst_ref=target, send_sem=send, recv_sem=recv, device_id=to, device_id_type=MESH
        )

    def piece(p, kinds):
        return pl.ds(p * (kinds // 4), kinds // 4)

    def send_x(step, j, kinds):
        pad = pads[step]
        for side, row, to_row, to, turns, by in (
            (0, j, rows + j, west, first_chip, X_CHIPS - 1),
            (1, rows - 1 - j, -1 - j, east, last_chip, 1 - X_CHIPS),
        ):

            def straight():
                remote(
                    pad.at[pl.ds(0, kinds), 2 + row, inside],
                    pad.at[pl.ds(0, kinds), 2 + to_row, inside],
                    x_send.at[step, side, j],
                    x_recv.at[step, side, j],
                    to,
                ).start()

            def round_about():
                for p in range(4):
                    if p < QUARTERS:
                        target, recv, device = detour.at[step, piece(p, kinds)], detour_recv.at[step, p], along(by)
                    else:
                        target, recv, device = pad.at[piece(p, kinds), 2 + to_row, inside], x_recv.at[step, side, j], to
                    remote(pad.at[piece(p, kinds), 2 + row, inside], target, x_send.at[step, side, j], recv, device).start()

            away = turns & (j == 0)
            pl.when(away)(round_about)
            pl.when(jnp.logical_not(away))(straight)

    def detour_copies(step, kinds):
        pad = pads[step]
        for here, side, to_row, by in ((first_chip, 1, -1, X_CHIPS), (last_chip, 0, rows, -X_CHIPS)):
            for p in range(QUARTERS):
                yield p, here, remote(
                    detour.at[step, piece(p, kinds)],
                    pad.at[piece(p, kinds), 2 + to_row, inside],
                    detour_send.at[step, p],
                    x_recv.at[step, side, 0],
                    along(by),
                ), remote(
                    detour.at[step, piece(p, kinds)],
                    detour.at[step, piece(p, kinds)],
                    detour_send.at[step, p],
                    detour_recv.at[step, p],
                    along(by),
                )

    def pass_on(step, wanted, kinds):
        for p, here, onward, arriving in detour_copies(step, kinds):
            if p == wanted:

                @pl.when(here)
                def _():
                    arriving.wait_recv()
                    onward.start()

    def end_x(step, j, kinds, sent):
        for side in range(2):
            block = pads[step].at[pl.ds(0, kinds), 2, inside]
            copy = remote(block, block, x_send.at[step, side, j], x_recv.at[step, side, j], east)
            copy.wait_send() if sent else copy.wait_recv()

    def y_copies(step, j, kinds):
        for group in (j, pairs - 1 - j):
            at = pl.ds(2 + 2 * group, 2)
            for side, first, to_first, to in ((0, EDGE, EDGE + cells_y, north), (1, EDGE + cells_y - 2, EDGE - 2, south)):
                yield side, remote(
                    pads[step].at[pl.ds(0, kinds), at, pl.ds(first, 2)],
                    pads[step].at[pl.ds(0, kinds), at, pl.ds(to_first, 2)],
                    y_send.at[step, side, group],
                    y_recv.at[step, side, group],
                    to,
                )

    def send_y(step, j, kinds):
        for side, copy in y_copies(step, j, kinds):
            pl.when(gy > 0 if side == 0 else gy < count_gy - 1)(copy.start)

    def end_y(step, j, kinds, sent):
        for side, copy in y_copies(step, j, kinds):
            if sent:
                pl.when(gy > 0 if side == 0 else gy < count_gy - 1)(copy.wait_send)
            else:
                pl.when(gy < count_gy - 1 if side == 0 else gy > 0)(copy.wait_recv)

    def vel_copy(step, row, source, to):
        return remote(source, vel.at[step, :, row], vel_send.at[step, row], vel_recv.at[step, row], {"comp": to})

    def send_vel(step, k):
        for row, to in ((k, 1), (rows - 1 - k, 3)):
            vel_copy(step, row, pads[step].at[pl.ds(0, 3), 2 + row, inside], to).start()

    def start(kinds, feeds):
        for j in range(2):
            loads[j].wait()
        for row in (0, rows - 1, 1, rows - 2):
            cover(row)
        pl.semaphore_wait(barrier, len(nearby))
        for j in range(2):
            send_x(0, j, kinds)
        if feeds:

            @pl.loop(0, pairs)
            def _(k):
                for row, to in ((k, 1), (rows - 1 - k, 3)):
                    vel_copy(0, row, state_ref.at[pl.ds(0, 3), row], to).start()

        send_y(0, 0, kinds)
        pl.when(gy == 0)(lambda: wall(0))
        pl.when(gy == count_gy - 1)(lambda: wall(EDGE + cells_y))
        loads[2].wait()

        @pl.loop(1, pairs // 2)
        def _(j):
            for k in (2 * j, 2 * j + 1):
                for row in (k, rows - 1 - k):
                    set_mask(row)
                    cover(row)
            send_y(0, j, kinds)

    def each_pair(kinds, first_pair, hand_on, compute, after):
        for step in range(ITERS):

            @pl.loop(0, pairs)
            def _(i):
                k = lax.rem(i + first_pair[step], pairs)
                odd = lax.rem(k, 2)

                for ready, p, at, when in hand_on:
                    if at == step:
                        pl.when(i == when)(lambda: pass_on(ready, p, kinds))

                @pl.when(k == 0)
                def _():
                    for j in range(2):
                        end_x(step, j, kinds, False)

                @pl.when(odd == 0)
                def _():
                    end_y(step, k // 2, kinds, False)

                compute(step, i, k)
                if step < ITERS - 1:
                    after(step + 1, k)
                    pl.when(k < 2)(lambda: send_x(step + 1, k, kinds))
                    pl.when(odd == 1)(lambda: send_y(step + 1, k // 2, kinds))

        for step in range(ITERS):
            for j in range(2):
                end_x(step, j, kinds, True)

            @pl.loop(0, pairs // 2)
            def _(j):
                end_y(step, j, kinds, True)

            for _, here, onward, _ in detour_copies(step, kinds):
                pl.when(here)(onward.wait_send)

    def cell(step, f, x, t, shift=0):
        return pads[step][f, x, pl.ds(EDGE + 8 * t + shift, 8)]

    def put(step, f, row, t, value):
        if step < ITERS:
            pads[step][f, 2 + row, pl.ds(EDGE + 8 * t, 8)] = value
        else:
            out_ref[f, row, pl.ds(8 * t, 8)] = value

    def density_slopes(step, row, at):
        x = row + 2
        scale = pressure_scale / 12.0

        def difference(f, t, along_x):
            if along_x:
                one, two = cell(step, f, x + 1, t) - cell(step, f, x - 1, t), cell(step, f, x + 2, t) - cell(step, f, x - 2, t)
            else:
                one, two = cell(step, f, x, t, 1) - cell(step, f, x, t, -1), cell(step, f, x, t, 2) - cell(step, f, x, t, -2)
            return 8.0 * one - two

        for t in range(tiles):
            for way, along_x in enumerate((True, False)):
                salt, heat = difference(3, t, along_x), difference(2, t, along_x)
                slope[pl.ds(at + (way * tiles + t) * 8, 8)] = (scale * haline_coef) * salt - (scale * thermal_coef) * heat

    def dynamics_row(step, row, at, beside):
        x = row + 2
        for t in range(tiles):
            u, v = cell(step, 0, x, t), cell(step, 1, x, t)
            m = mask[row, pl.ds(8 * t, 8)]
            along_x, along_y = weights(u, 1.0), weights(v, 1.0)
            middle = -0.5 * (jnp.abs(u) + jnp.abs(v)) - (4.0 * lateral_mix + 2.0 * vertical_mix)
            y = gy * cells_y + 8 * t + lax.broadcasted_iota(jnp.int32, (8, depth), 0)
            latitude = 2.0 * y.astype(jnp.float32) / float(cells_y * count_gy - 1) - 1.0
            spin = coriolis_mean + coriolis_slope * latitude
            for f in (2, 3, 0, 1):
                q = cell(step, f, x, t)
                total = middle * q + beside(q)
                for w, shift in zip(along_x, (1, -1, 2, -2)):
                    total += w * cell(step, f, x + shift, t)
                for w, shift in zip(along_y, (1, -1, 2, -2)):
                    total += w * cell(step, f, x, t, shift)
                if f == 0:
                    total += spin * v - push[pl.ds(at + t * 8, 8)]
                if f == 1:
                    total -= spin * u + push[pl.ds(at + (tiles + t) * 8, 8)]
                before = cell(step, 4 + f, x, t)
                put(step + 1, f, row, t, m * (q + ((1.5 * time_step) * total - (0.5 * time_step) * before)))
                put(step + 1, 4 + f, row, t, m * total)

    def run_dynamics():
        above = lax.rem(lax.broadcasted_iota(jnp.int32, (2 * depth, depth), 0), depth)
        below = lax.broadcasted_iota(jnp.int32, (2 * depth, depth), 1)
        summing[...] = jnp.where(above <= below, 1.0, 0.0).astype(jnp.bfloat16)
        start(4, True)
        beside = neighbours_above_below(vertical_mix)

        def compute(step, i, k):
            density_slopes(step, k, 0)
            density_slopes(step, rows - 1 - k, 2 * cells_y)
            high, low = halves(slope[...])
            push[...] = jnp.dot(
                jnp.concatenate([high, low], axis=1), summing[...], preferred_element_type=jnp.float32
            )
            dynamics_row(step, k, 0, beside)
            dynamics_row(step, rows - 1 - k, 2 * cells_y, beside)

        each_pair(4, [pairs // 2] * ITERS, [(step, p, step, pairs // 2) for step in range(ITERS) for p in range(QUARTERS)], compute, send_vel)

        @pl.loop(0, ITERS)
        def _(step):
            @pl.loop(0, rows)
            def _(row):
                vel_copy(step, row, vel.at[step, :, row], 1).wait_send()

    def react(step, row, at):
        for t in range(0, tiles, 2):
            parts = []
            for tile in (t, t + 1):
                q = pads[step][:, row + 2, pl.ds(EDGE + 8 * tile, 8)].reshape(8 * fields, depth)
                high, low = halves(q)
                parts.append(jnp.concatenate([high, low, high], axis=0))
            rates[at + t // 2] = jnp.dot(
                mixing[...], jnp.concatenate(parts, axis=1), preferred_element_type=jnp.float32
            )

    def tracer_row(step, row, at, beside):
        x = row + 2
        for t in range(tiles):
            here = pl.ds(8 * t, 8)
            u, v, heat = vel[step, 0, row, here], vel[step, 1, row, here], vel[step, 2, row, here]
            m = mask[row, here]
            along_x, along_y = weights(u, time_step), weights(v, time_step)
            middle = (-0.5 * time_step) * (jnp.abs(u) + jnp.abs(v)) + (
                1.0 - time_step * (4.0 * lateral_mix + 2.0 * vertical_mix)
            )
            growth = (2.0 * time_step) * jax.nn.sigmoid(heat)
            for f in range(fields):
                q = cell(step, f, x, t)
                total = middle * q + growth * rates[at + t // 2, pl.ds(8 * f, 8), pl.ds((t % 2) * depth, depth)]
                for w, shift in zip(along_x, (1, -1, 2, -2)):
                    total += w * cell(step, f, x + shift, t)
                for w, shift in zip(along_y, (1, -1, 2, -2)):
                    total += w * cell(step, f, x, t, shift)
                total += beside(q)
                put(step + 1, f, row, t, m * total)

    def run_tracers():
        column = lax.broadcasted_iota(jnp.int32, (8, 3 * 8 * fields), 1)
        same = lax.rem(column, 8) == lax.broadcasted_iota(jnp.int32, (8, 3 * 8 * fields), 0)
        source = lax.rem(column, 8 * fields) // 8
        blocks = []
        for i in range(fields):
            block = jnp.zeros((8, 3 * 8 * fields), jnp.float32)
            for j in range(fields):
                block = jnp.where(same & (source == j), coupling[slot - 1, i, j], block)
            high = block.astype(jnp.bfloat16).astype(jnp.float32)
            blocks.append(jnp.where(column < 2 * 8 * fields, high, block - high))
        mixing[...] = jnp.concatenate(blocks, axis=0).astype(jnp.bfloat16)
        start(fields, False)
        beside = neighbours_above_below(time_step * vertical_mix)
        total = ITERS * pairs
        ahead = LAG * (3 - slot) // 2
        behind = LAG * (slot - 1) // 2

        def relay(c, up, last, to):
            step = c // pairs
            k = (c + (step + 2) // 3 * (pairs // 2)) % pairs
            row = k if up else rows - 1 - k
            copy = vel_copy(step, row, vel.at[step, :, row], to)
            copy.wait_recv()
            pl.when(last)(copy.start)

        def going_up(c):
            relay(c, True, slot < 3, lax.rem(slot + 1, 4))

        def going_down(c):
            relay(c, False, slot > 1, slot - 1)

        @pl.loop(0, ahead)
        def _(c):
            going_up(c)

        @pl.loop(0, behind)
        def _(c):
            going_down(c)

        def compute(step, i, k):
            react(step, k, 0)
            react(step, rows - 1 - k, tiles // 2)
            n = step * pairs + i
            pl.when(n + ahead < total)(lambda: going_up(n + ahead))
            tracer_row(step, k, 0, beside)
            pl.when(n + behind < total)(lambda: going_down(n + behind))
            tracer_row(step, rows - 1 - k, tiles // 2, beside)

        each_pair(fields, [0] + [pairs // 2] * (ITERS - 1), HAND_ON, compute, lambda step, k: None)

        @pl.loop(0, total)
        def _(c):
            step = c // pairs
            k = c % pairs
            pl.when(slot < 3)(lambda: vel_copy(step, k, vel.at[step, :, k], 1).wait_send())
            pl.when(slot > 1)(lambda: vel_copy(step, rows - 1 - k, vel.at[step, :, k], 1).wait_send())

    pl.when(slot == 0)(run_dynamics)
    pl.when(slot != 0)(run_tracers)


def solution(mesh):
    mesh_size = (mesh.shape["gx"], mesh.shape["gy"])

    def per_device(state, levels, reaction):
        fields, rows, cells_y, depth = state.shape
        dma = pltpu.SemaphoreType.DMA
        padded = (fields, rows + 4, cells_y + 2 * EDGE, depth)
        return pl.pallas_call(
            functools.partial(kernel, mesh_size),
            out_shape=jax.ShapeDtypeStruct(state.shape, state.dtype),
            in_specs=[pl.BlockSpec(memory_space=pltpu.HBM)] * 3,
            out_specs=pl.BlockSpec(memory_space=pltpu.VMEM),
            scratch_shapes=[
                *[pltpu.VMEM(padded, jnp.float32)] * ITERS,
                pltpu.VMEM((ITERS, 3, rows, cells_y, depth), jnp.float32),
                pltpu.VMEM((rows, cells_y, depth), jnp.float32),
                pltpu.VMEM(levels.shape, jnp.int32),
                pltpu.VMEM((8 * fields, 3 * 8 * fields), jnp.bfloat16),
                pltpu.VMEM((cells_y // 8, 8 * fields, 2 * depth), jnp.float32),
                pltpu.VMEM((2 * depth, depth), jnp.bfloat16),
                pltpu.VMEM((4 * cells_y, depth), jnp.float32),
                pltpu.VMEM((4 * cells_y, depth), jnp.float32),
                pltpu.VMEM((ITERS, fields, cells_y, depth), jnp.float32),
                pltpu.SMEM(reaction.shape, jnp.float32),
                dma((5,)),
                dma((ITERS, rows)),
                dma((ITERS, rows)),
                dma((ITERS, 2, 2)),
                dma((ITERS, 2, 2)),
                dma((ITERS, 2, rows // 2)),
                dma((ITERS, 2, rows // 2)),
                dma((ITERS, QUARTERS)),
                dma((ITERS, QUARTERS)),
            ],
            compiler_params=pltpu.CompilerParams(
                collective_id=0, has_side_effects=True, vmem_limit_bytes=40 * 1024 * 1024
            ),
        )(*[pltpu.with_memory_space_constraint(a, pltpu.HBM) for a in (state, levels, reaction)])

    in_specs = (P("comp", "gx", "gy", None), P("gx", "gy"), P())
    out_specs = P("comp", "gx", "gy", None)
    return jax.shard_map(per_device, mesh=mesh, in_specs=in_specs, out_specs=out_specs, check_vma=False)
```

```python
import functools

import jax
import jax.numpy as jnp
from jax import lax
from jax.experimental import pallas as pl
from jax.experimental.pallas import tpu as pltpu
from jax.sharding import PartitionSpec as P

MESH = pl.DeviceIdType.MESH
ITERS = 3
EDGE = 8
X_CHIPS = 4
LAG = 8
QUARTERS = 3
HAND_ON = tuple((0, p, 0, 0) for p in range(QUARTERS)) + ((1, 0, 0, 4), (1, 1, 0, 5), (1, 2, 0, 6), (2, 0, 2, 0), (2, 1, 2, 1), (2, 2, 2, 2))

time_step = 0.25
lateral_mix = 0.05
vertical_mix = 0.1
pressure_scale = 0.05
thermal_coef = 1.0
haline_coef = 0.8
coriolis_mean = 0.5
coriolis_slope = 0.5


def weights(speed, scale):
    size = jnp.abs(speed)
    mix = scale * lateral_mix
    eight = speed * (scale * 8.0 / 12.0)
    four = size * (scale * 4.0 / 12.0) + mix
    return four - eight, four + eight, (speed - size) * (scale / 12.0), (speed + size) * (-scale / 12.0)


def halves(value):
    high = value.astype(jnp.bfloat16)
    return high, (value - high.astype(jnp.float32)).astype(jnp.bfloat16)


def kernel(
    mesh_size, state_ref, levels_ref, reaction_ref, out_ref, pad0, pad1, pad2, vel, mask, level, mixing, rates, summing, slope,
    push, detour, coupling, load_sem, vel_send, vel_recv, x_send, x_recv, y_send, y_recv, detour_recv, detour_send,
):
    count_gx, count_gy = mesh_size
    pads = (pad0, pad1, pad2)
    fields, rows, cells_y, depth = state_ref.shape
    pairs = rows // 2
    tiles = cells_y // 8
    slot = lax.axis_index("comp")
    gx = lax.axis_index("gx")
    gy = lax.axis_index("gy")

    def along(by):
        return {"gx": lax.rem(gx + (count_gx + by), count_gx)}

    east, west = along(1), along(-1)
    south = {"gy": lax.rem(gy + 1, count_gy)}
    north = {"gy": lax.rem(gy + count_gy - 1, count_gy)}
    chip = lax.rem(gx, X_CHIPS)
    first_chip, last_chip = chip == 0, chip == X_CHIPS - 1
    inside = pl.ds(EDGE, cells_y)

    def load(j, first, size):
        return pltpu.make_async_copy(
            state_ref.at[:, pl.ds(first, size)], pad0.at[:, pl.ds(2 + first, size), inside], load_sem.at[j]
        )

    loads = [load(0, 0, 2), load(1, rows - 2, 2), load(2, 2, rows - 4)]
    small = [
        pltpu.make_async_copy(levels_ref, level, load_sem.at[3]),
        pltpu.make_async_copy(reaction_ref, coupling, load_sem.at[4]),
    ]
    for copy in small + loads:
        copy.start()

    barrier = pltpu.get_barrier_semaphore()
    nearby = [along(by) for by in (1, -1, X_CHIPS, -X_CHIPS, X_CHIPS - 1, 1 - X_CHIPS)]
    nearby += [south, north, {"comp": lax.rem(slot + 1, 4)}, {"comp": lax.rem(slot + 3, 4)}]
    for near in nearby:
        pl.semaphore_signal(barrier, inc=1, device_id=near, device_id_type=MESH)

    lane = lax.broadcasted_iota(jnp.int32, (8, depth), 1)
    own_y = lax.broadcasted_iota(jnp.int32, (8, cells_y), 0)
    at_y = lax.broadcasted_iota(jnp.int32, (8, cells_y), 1)
    lanes = lane.astype(jnp.float32)
    def set_mask(row):
        here = jnp.broadcast_to(level[pl.ds(row, 1), :], (8, cells_y)).astype(jnp.float32)
        for t in range(tiles):
            column = jnp.sum(jnp.where(at_y == own_y + 8 * t, here, 0.0), axis=1, keepdims=True)
            mask[row, pl.ds(8 * t, 8)] = jnp.where(lanes < column, 1.0, 0.0)

    for copy in small:
        copy.wait()
    for row in (0, rows - 1, 1, rows - 2):
        set_mask(row)

    def wall(first):
        zeros = jnp.zeros((8, depth), jnp.float32)

        @pl.loop(0, rows)
        def _(row):
            for pad in pads:
                for f in range(fields):
                    pad[f, 2 + row, pl.ds(first, 8)] = zeros

    def neighbours_above_below(scale):
        up = jnp.where(lane > 0, scale, 0.0)
        down = jnp.where(lane < depth - 1, scale, 0.0)
        return lambda q: up * pltpu.roll(q, 1, 1) + down * pltpu.roll(q, depth - 1, 1)

    def cover(row):
        for f in range(fields):
            pad0[f, 2 + row, inside] = pad0[f, 2 + row, inside] * mask[row]

    def remote(source, target, send, recv, to):
        return pltpu.make_async_remote_copy(
            src_ref=source, dst_ref=target, send_sem=send, recv_sem=recv, device_id=to, device_id_type=MESH
        )

    def piece(p, kinds):
        return pl.ds(p * (kinds // 4), kinds // 4)

    def send_x(step, j, kinds):
        pad = pads[step]
        for side, row, to_row, to, turns, by in (
            (0, j, rows + j, west, first_chip, X_CHIPS - 1),
            (1, rows - 1 - j, -1 - j, east, last_chip, 1 - X_CHIPS),
        ):

            def straight():
                remote(
                    pad.at[pl.ds(0, kinds), 2 + row, inside],
                    pad.at[pl.ds(0, kinds), 2 + to_row, inside],
                    x_send.at[step, side, j],
                    x_recv.at[step, side, j],
                    to,
                ).start()

            def round_about():
                for p in range(4):
                    if p < QUARTERS:
                        target, recv, device = detour.at[step, piece(p, kinds)], detour_recv.at[step, p], along(by)
                    else:
                        target, recv, device = pad.at[piece(p, kinds), 2 + to_row, inside], x_recv.at[step, side, j], to
                    remote(pad.at[piece(p, kinds), 2 + row, inside], target, x_send.at[step, side, j], recv, device).start()

            away = turns & (j == 0)
            pl.when(away)(round_about)
            pl.when(jnp.logical_not(away))(straight)

    def detour_copies(step, kinds):
        pad = pads[step]
        for here, side, to_row, by in ((first_chip, 1, -1, X_CHIPS), (last_chip, 0, rows, -X_CHIPS)):
            for p in range(QUARTERS):
                yield p, here, remote(
                    detour.at[step, piece(p, kinds)],
                    pad.at[piece(p, kinds), 2 + to_row, inside],
                    detour_send.at[step, p],
                    x_recv.at[step, side, 0],
                    along(by),
                ), remote(
                    detour.at[step, piece(p, kinds)],
                    detour.at[step, piece(p, kinds)],
                    detour_send.at[step, p],
                    detour_recv.at[step, p],
                    along(by),
                )

    def pass_on(step, wanted, kinds):
        for p, here, onward, arriving in detour_copies(step, kinds):
            if p == wanted:

                @pl.when(here)
                def _():
                    arriving.wait_recv()
                    onward.start()

    def end_x(step, j, kinds, sent):
        for side in range(2):
            block = pads[step].at[pl.ds(0, kinds), 2, inside]
            copy = remote(block, block, x_send.at[step, side, j], x_recv.at[step, side, j], east)
            copy.wait_send() if sent else copy.wait_recv()

    def y_copies(step, j, kinds):
        for group in (j, pairs - 1 - j):
            at = pl.ds(2 + 2 * group, 2)
            for side, first, to_first, to in ((0, EDGE, EDGE + cells_y, north), (1, EDGE + cells_y - 2, EDGE - 2, south)):
                yield side, remote(
                    pads[step].at[pl.ds(0, kinds), at, pl.ds(first, 2)],
                    pads[step].at[pl.ds(0, kinds), at, pl.ds(to_first, 2)],
                    y_send.at[step, side, group],
                    y_recv.at[step, side, group],
                    to,
                )

    def send_y(step, j, kinds):
        for side, copy in y_copies(step, j, kinds):
            pl.when(gy > 0 if side == 0 else gy < count_gy - 1)(copy.start)

    def end_y(step, j, kinds, sent):
        for side, copy in y_copies(step, j, kinds):
            if sent:
                pl.when(gy > 0 if side == 0 else gy < count_gy - 1)(copy.wait_send)
            else:
                pl.when(gy < count_gy - 1 if side == 0 else gy > 0)(copy.wait_recv)

    def vel_copy(step, row, source, to):
        return remote(source, vel.at[step, :, row], vel_send.at[step, row], vel_recv.at[step, row], {"comp": to})

    def send_vel(step, k):
        for row, to in ((k, 1), (rows - 1 - k, 3)):
            vel_copy(step, row, pads[step].at[pl.ds(0, 3), 2 + row, inside], to).start()

    def start(kinds, feeds):
        if not feeds:
            for j in range(2):
                loads[j].wait()
            for row in (0, rows - 1, 1, rows - 2):
                cover(row)
        pl.semaphore_wait(barrier, len(nearby))
        if feeds:

            @pl.loop(0, pairs)
            def _(k):
                for row, to in ((k, 1), (rows - 1 - k, 3)):
                    vel_copy(0, row, state_ref.at[pl.ds(0, 3), row], to).start()

            for j in range(2):
                loads[j].wait()
            for row in (0, rows - 1, 1, rows - 2):
                cover(row)
        for j in range(2):
            send_x(0, j, kinds)
        send_y(0, 0, kinds)
        pl.when(gy == 0)(lambda: wall(0))
        pl.when(gy == count_gy - 1)(lambda: wall(EDGE + cells_y))
        loads[2].wait()

        @pl.loop(1, pairs // 2)
        def _(j):
            for k in (2 * j, 2 * j + 1):
                for row in (k, rows - 1 - k):
                    set_mask(row)
                    cover(row)
            send_y(0, j, kinds)

    def order(kind, i):
        half = pairs // 4
        group = i // 2
        late = group // half
        inwards = group
        middle = (group + half) % (2 * half)
        outwards = (1 - late) * (group + half) + late * (2 * half - 1 - group)
        chosen = (1 - kind) * (2 - kind) // 2 * inwards + kind * (2 - kind) * middle + kind * (kind - 1) // 2 * outwards
        return 2 * chosen + i % 2

    def each_pair(kinds, orders, hand_on, prepare, compute, after):
        for step in range(ITERS):

            @pl.loop(0, pairs)
            def _(i):
                k = order(orders[step], i)
                odd = lax.rem(k, 2)
                prepare(step, k)

                for ready, p, at, when in hand_on:
                    if at == step:
                        pl.when(i == when)(lambda: pass_on(ready, p, kinds))

                @pl.when(k == 0)
                def _():
                    for j in range(2):
                        end_x(step, j, kinds, False)

                @pl.when(odd == 0)
                def _():
                    end_y(step, k // 2, kinds, False)

                compute(step, i, k)
                if step < ITERS - 1:
                    after(step + 1, k)
                    pl.when(k < 2)(lambda: send_x(step + 1, k, kinds))
                    pl.when(odd == 1)(lambda: send_y(step + 1, k // 2, kinds))

        for step in range(ITERS):
            for j in range(2):
                end_x(step, j, kinds, True)

            @pl.loop(0, pairs // 2)
            def _(j):
                end_y(step, j, kinds, True)

            for _, here, onward, _ in detour_copies(step, kinds):
                pl.when(here)(onward.wait_send)

    def cell(step, f, x, t, shift=0):
        return pads[step][f, x, pl.ds(EDGE + 8 * t + shift, 8)]

    def put(step, f, row, t, value):
        if step < ITERS:
            pads[step][f, 2 + row, pl.ds(EDGE + 8 * t, 8)] = value
        else:
            out_ref[f, row, pl.ds(8 * t, 8)] = value

    def density_slopes(step, row, at):
        x = row + 2
        scale = pressure_scale / 12.0

        def difference(f, t, along_x):
            if along_x:
                one, two = cell(step, f, x + 1, t) - cell(step, f, x - 1, t), cell(step, f, x + 2, t) - cell(step, f, x - 2, t)
            else:
                one, two = cell(step, f, x, t, 1) - cell(step, f, x, t, -1), cell(step, f, x, t, 2) - cell(step, f, x, t, -2)
            return 8.0 * one - two

        for t in range(tiles):
            for way, along_x in enumerate((True, False)):
                salt, heat = difference(3, t, along_x), difference(2, t, along_x)
                slope[pl.ds(at + (way * tiles + t) * 8, 8)] = (scale * haline_coef) * salt - (scale * thermal_coef) * heat

    def dynamics_row(step, row, at, beside):
        x = row + 2
        for t in range(tiles):
            u, v = cell(step, 0, x, t), cell(step, 1, x, t)
            m = mask[row, pl.ds(8 * t, 8)]
            along_x, along_y = weights(u, 1.0), weights(v, 1.0)
            middle = -0.5 * (jnp.abs(u) + jnp.abs(v)) - (4.0 * lateral_mix + 2.0 * vertical_mix)
            y = gy * cells_y + 8 * t + lax.broadcasted_iota(jnp.int32, (8, depth), 0)
            latitude = 2.0 * y.astype(jnp.float32) / float(cells_y * count_gy - 1) - 1.0
            spin = coriolis_mean + coriolis_slope * latitude
            for f in (2, 3, 0, 1):
                q = cell(step, f, x, t)
                total = middle * q + beside(q)
                for w, shift in zip(along_x, (1, -1, 2, -2)):
                    total += w * cell(step, f, x + shift, t)
                for w, shift in zip(along_y, (1, -1, 2, -2)):
                    total += w * cell(step, f, x, t, shift)
                if f == 0:
                    total += spin * v - push[pl.ds(at + t * 8, 8)]
                if f == 1:
                    total -= spin * u + push[pl.ds(at + (tiles + t) * 8, 8)]
                before = cell(step, 4 + f, x, t)
                put(step + 1, f, row, t, m * (q + ((1.5 * time_step) * total - (0.5 * time_step) * before)))
                put(step + 1, 4 + f, row, t, m * total)

    def run_dynamics():
        above = lax.rem(lax.broadcasted_iota(jnp.int32, (2 * depth, depth), 0), depth)
        below = lax.broadcasted_iota(jnp.int32, (2 * depth, depth), 1)
        summing[...] = jnp.where(above <= below, 1.0, 0.0).astype(jnp.bfloat16)
        start(4, True)
        beside = neighbours_above_below(vertical_mix)

        def compute(step, i, k):
            density_slopes(step, k, 0)
            density_slopes(step, rows - 1 - k, 2 * cells_y)
            high, low = halves(slope[...])
            push[...] = jnp.dot(
                jnp.concatenate([high, low], axis=1), summing[...], preferred_element_type=jnp.float32
            )
            dynamics_row(step, k, 0, beside)
            dynamics_row(step, rows - 1 - k, 2 * cells_y, beside)

        each_pair(4, [1, 2, 2], [(step, p, step, (4, 6, 6)[step]) for step in range(ITERS) for p in range(QUARTERS)], lambda step, k: None, compute, send_vel)

        @pl.loop(0, ITERS)
        def _(step):
            @pl.loop(0, rows)
            def _(row):
                vel_copy(step, row, vel.at[step, :, row], 1).wait_send()

    def react(step, row, at):
        for t in range(0, tiles, 2):
            parts = []
            for tile in (t, t + 1):
                q = pads[step][:, row + 2, pl.ds(EDGE + 8 * tile, 8)].reshape(8 * fields, depth)
                high, low = halves(q)
                parts.append(jnp.concatenate([high, low, high], axis=0))
            rates[at + t // 2] = jnp.dot(
                mixing[...], jnp.concatenate(parts, axis=1), preferred_element_type=jnp.float32
            )

    def tracer_row(step, row, at, beside):
        x = row + 2
        for t in range(tiles):
            here = pl.ds(8 * t, 8)
            u, v, heat = vel[step, 0, row, here], vel[step, 1, row, here], vel[step, 2, row, here]
            m = mask[row, here]
            along_x, along_y = weights(u, time_step), weights(v, time_step)
            middle = (-0.5 * time_step) * (jnp.abs(u) + jnp.abs(v)) + (
                1.0 - time_step * (4.0 * lateral_mix + 2.0 * vertical_mix)
            )
            growth = (2.0 * time_step) * jax.nn.sigmoid(heat)
            for f in range(fields):
                q = cell(step, f, x, t)
                total = middle * q + growth * rates[at + t // 2, pl.ds(8 * f, 8), pl.ds((t % 2) * depth, depth)]
                for w, shift in zip(along_x, (1, -1, 2, -2)):
                    total += w * cell(step, f, x + shift, t)
                for w, shift in zip(along_y, (1, -1, 2, -2)):
                    total += w * cell(step, f, x, t, shift)
                total += beside(q)
                put(step + 1, f, row, t, m * total)

    def run_tracers():
        start(fields, False)
        column = lax.broadcasted_iota(jnp.int32, (8, 3 * 8 * fields), 1)
        same = lax.rem(column, 8) == lax.broadcasted_iota(jnp.int32, (8, 3 * 8 * fields), 0)
        source = lax.rem(column, 8 * fields) // 8
        blocks = []
        for i in range(fields):
            block = jnp.zeros((8, 3 * 8 * fields), jnp.float32)
            for j in range(fields):
                block = jnp.where(same & (source == j), coupling[slot - 1, i, j], block)
            high = block.astype(jnp.bfloat16).astype(jnp.float32)
            blocks.append(jnp.where(column < 2 * 8 * fields, high, block - high))
        mixing[...] = jnp.concatenate(blocks, axis=0).astype(jnp.bfloat16)
        beside = neighbours_above_below(time_step * vertical_mix)
        total = ITERS * pairs
        ahead = LAG * (3 - slot) // 2
        behind = LAG * (slot - 1) // 2

        def relay(c, up, last, to):
            step = c // pairs
            k = order(step, c % pairs)
            row = k if up else rows - 1 - k
            copy = vel_copy(step, row, vel.at[step, :, row], to)
            copy.wait_recv()
            pl.when(last)(copy.start)

        def going_up(c):
            relay(c, True, slot < 3, lax.rem(slot + 1, 4))

        def going_down(c):
            relay(c, False, slot > 1, slot - 1)

        @pl.loop(0, ahead)
        def _(c):
            going_up(c)

        @pl.loop(0, behind)
        def _(c):
            going_down(c)

        def prepare(step, k):
            react(step, k, 0)
            react(step, rows - 1 - k, tiles // 2)

        def compute(step, i, k):
            n = step * pairs + i
            pl.when(n + ahead < total)(lambda: going_up(n + ahead))
            tracer_row(step, k, 0, beside)
            pl.when(n + behind < total)(lambda: going_down(n + behind))
            tracer_row(step, rows - 1 - k, tiles // 2, beside)

        each_pair(fields, [0, 1, 2], HAND_ON, prepare, compute, lambda step, k: None)

        @pl.loop(0, total)
        def _(c):
            step = c // pairs
            k = c % pairs
            pl.when(slot < 3)(lambda: vel_copy(step, k, vel.at[step, :, k], 1).wait_send())
            pl.when(slot > 1)(lambda: vel_copy(step, rows - 1 - k, vel.at[step, :, k], 1).wait_send())

    pl.when(slot == 0)(run_dynamics)
    pl.when(slot != 0)(run_tracers)


def solution(mesh):
    mesh_size = (mesh.shape["gx"], mesh.shape["gy"])

    def per_device(state, levels, reaction):
        fields, rows, cells_y, depth = state.shape
        dma = pltpu.SemaphoreType.DMA
        padded = (fields, rows + 4, cells_y + 2 * EDGE, depth)
        return pl.pallas_call(
            functools.partial(kernel, mesh_size),
            out_shape=jax.ShapeDtypeStruct(state.shape, state.dtype),
            in_specs=[pl.BlockSpec(memory_space=pltpu.HBM)] * 3,
            out_specs=pl.BlockSpec(memory_space=pltpu.VMEM),
            scratch_shapes=[
                *[pltpu.VMEM(padded, jnp.float32)] * ITERS,
                pltpu.VMEM((ITERS, 3, rows, cells_y, depth), jnp.float32),
                pltpu.VMEM((rows, cells_y, depth), jnp.float32),
                pltpu.VMEM(levels.shape, jnp.int32),
                pltpu.VMEM((8 * fields, 3 * 8 * fields), jnp.bfloat16),
                pltpu.VMEM((cells_y // 8, 8 * fields, 2 * depth), jnp.float32),
                pltpu.VMEM((2 * depth, depth), jnp.bfloat16),
                pltpu.VMEM((4 * cells_y, depth), jnp.float32),
                pltpu.VMEM((4 * cells_y, depth), jnp.float32),
                pltpu.VMEM((ITERS, fields, cells_y, depth), jnp.float32),
                pltpu.SMEM(reaction.shape, jnp.float32),
                dma((5,)),
                dma((ITERS, rows)),
                dma((ITERS, rows)),
                dma((ITERS, 2, 2)),
                dma((ITERS, 2, 2)),
                dma((ITERS, 2, rows // 2)),
                dma((ITERS, 2, rows // 2)),
                dma((ITERS, QUARTERS)),
                dma((ITERS, QUARTERS)),
            ],
            compiler_params=pltpu.CompilerParams(
                collective_id=0, has_side_effects=True, vmem_limit_bytes=40 * 1024 * 1024
            ),
        )(*[pltpu.with_memory_space_constraint(a, pltpu.HBM) for a in (state, levels, reaction)])

    in_specs = (P("comp", "gx", "gy", None), P("gx", "gy"), P())
    out_specs = P("comp", "gx", "gy", None)
    return jax.shard_map(per_device, mesh=mesh, in_specs=in_specs, out_specs=out_specs, check_vma=False)
```
